512 devices in a mesh: dp: 32 (over x, y), tensor: 16 (over z, core).
Axes of the slice: x: 4, y: 8, z: 8, core: 2. Of those that a mesh axis runs over, the one named last changes fastest.
Arguments:
- acts: bfloat16 [4096, 4096], P('dp'), may hold values from -6 to 6
- grad_out: bfloat16 [4096, 14336], P('dp', 'tensor'), may hold values from -0.09375 to 0.09375
- selected: int32 [16, 1], P('tensor'), may hold values from 0 to 6, as said below
- owner: int32 [16, 192, 1], P('tensor'), may hold values from 0 to 31; in each aligned block of 192 rows (0 to 191, 192 to 383, ..., all dimensions but the last counted through in order) at most 9 rows name the same one
- sel_weight: float32 [4096, 2048], P('dp', 'tensor'), may hold values from -3 to 3
- sel_moment: float32 [4096, 2048], P('dp', 'tensor'), may hold values from -3 to 3
- sel_second: float32 [4096, 2048], P('dp', 'tensor'), may hold values from 0.01 to 1
- off_weight: float32 [32, 16, 9, 128, 128], P('dp', 'tensor'), may hold values from -3 to 3
- off_moment: float32 [32, 16, 9, 128, 128], P('dp', 'tensor'), may hold values from -3 to 3
- off_second: float32 [32, 16, 9, 128, 128], P('dp', 'tensor'), may hold values from 0.01 to 1
Outputs:
- column_norm: float32 [14336], P('tensor')
- sel_weight_new: float32 [4096, 2048], P('dp', 'tensor')
- sel_moment_new: float32 [4096, 2048], P('dp', 'tensor')
- sel_second_new: float32 [4096, 2048], P('dp', 'tensor')
- off_weight_new: float32 [32, 16, 9, 128, 128], P('dp', 'tensor')
- off_moment_new: float32 [32, 16, 9, 128, 128], P('dp', 'tensor')
- off_second_new: float32 [32, 16, 9, 128, 128], P('dp', 'tensor')
The draws below stay inside these ranges and needn't reach their ends.
Inputs may be any that keep to these rules, and one draw needn't show every extreme that they name: `selected`: each row names 1 tile. For each index of tensor, no owner receives more than 9 pieces, and some owner receives exactly 9.
All inputs are finite; a program needn't handle non-finite values.
Results may differ from the reference program's by a relative error of at most 0.0017.
Values may be sent and summed in bfloat16 or wider, within the bound.
No kernel may reach another device: no remote copies, remote signals or barrier semaphores. Data moves between devices by JAX's collectives and lax.ppermute only.
A program may use at most 128 MiB of HBM per device.

```python
import math
import jax
import jax.numpy as jnp
import numpy as np
from jax import lax

ROWS = 4096
FFW = 14336
TILE = 128
TOK_DEV = 128
TOKENS = 4096
TILES_DEV = 7
SEL_TILES = 1
REST_TILES = 6
BLOCK_ROWS = 128
PIECES = 192
CAP = 9
N_DP = 32
N_TENSOR = 16


def draw_selected(key, part):
    row_keys = jax.random.split(jax.random.fold_in(key, 17), N_TENSOR)
    shuffled = jax.vmap(lambda row_key: jax.random.permutation(row_key, TILES_DEV))(row_keys)
    return jnp.sort(shuffled[:, :SEL_TILES], axis=1).astype(jnp.int32)


def shard_levels(key, extent, cuts, low, high):
    def one(axis_at, parts):
        heights = jax.random.uniform(jax.random.fold_in(jax.random.fold_in(key, 6), axis_at), (parts,), jnp.float32, low / len(cuts), high / len(cuts))
        return jnp.repeat(jnp.exp(heights), extent[axis_at] // parts).reshape((-1,) + (1,) * (len(extent) - axis_at - 1))

    factor_of = one(*cuts[0])
    for cut in cuts[1:]:
        factor_of = factor_of * one(*cut)
    return factor_of


def deal_out(own_key, own, number, rows, amount, top, bound, slope):
    order = jax.random.permutation(own_key, amount)
    crowded, usual = shares(amount, rows * top, bound, slope, True), shares(amount, rows * top, bound, slope, False)
    places = jnp.arange(amount)

    def named(lengths, rotation):
        used = int((lengths > 0).sum())
        fixed = max(1, used // 4)
        shifted = fixed + (places - fixed + rotation * (used - fixed)) % max(1, amount - fixed)
        return jnp.zeros((amount,), jnp.int32).at[order[jnp.where(places < fixed, places, shifted)]].set(jnp.asarray(lengths, jnp.int32))

    lengths = jnp.where(number % 4 == 0, named(crowded, number // 4), named(usual, number - number // 4 - 1))
    mixed = jax.random.permutation(jax.random.fold_in(own, 3), amount)
    giver, receiver = mixed[0:amount // 2 * 2:2], mixed[1:amount // 2 * 2:2]
    slack = jnp.minimum(lengths[giver] - 1, bound - lengths[receiver]) // 2
    slack = jnp.where((giver == order[0]) | (receiver == order[0]) | (lengths[receiver] == 0), 0, jnp.maximum(slack, 0))
    shifted = jax.random.randint(jax.random.fold_in(own, 4), (amount // 2,), 0, 1 << 20) % (slack + 1)
    lengths = lengths.at[giver].add(-shifted).at[receiver].add(shifted)
    members = jnp.searchsorted(jnp.cumsum(lengths), jnp.arange(rows * top), side="right").astype(jnp.int32)
    table = members.reshape(top, rows).T
    table = table[jax.random.permutation(jax.random.fold_in(own, 1), rows)]
    rotation = jax.random.randint(jax.random.fold_in(own, 2), (rows, 1), 0, top)
    return jnp.take_along_axis(table, (jnp.arange(top)[None, :] + rotation) % top, axis=1)


def shares(amount, total, bound, skew, full):
    loads = [(1 << 20) // math.isqrt(grade ** skew) + 1 for grade in range(1, amount + 1)]
    largest = bound if full else min(bound, max(-(-total // amount), total * loads[0] // sum(loads)))
    least = 1 if total - largest >= amount - 1 else 0
    given, rest = [largest] + [least] * (amount - 1), total - largest - least * (amount - 1)
    while rest > 0:
        movable = [i for i in range(1, amount) if given[i] < largest] or [i for i in range(1, amount) if given[i] < bound]
        whole, left = sum([loads[i] for i in movable]), rest
        for i in movable:
            extra = min(bound - given[i], max(1, left * loads[i] // whole), rest)
            given[i] = given[i] + extra
            rest = rest - extra
    return np.array(given)


def centred(rng, dims, deviation, bound, cuts=(), kind=jnp.bfloat16):
    entries = deviation * jax.random.normal(rng, dims, jnp.float32)
    if cuts:
        entries = entries * shard_levels(rng, dims, cuts, -0.22, 0.18)
    return jnp.clip(entries, -bound, bound).astype(kind)


def setup_inputs(seed: int = 0) -> dict:
    keys = jax.random.split(jax.random.key(seed), 11)
    acts = centred(keys[0], (TOKENS, ROWS), 1.0, 6.0, ((0, 32),))
    grad_out = centred(keys[1], (TOKENS, FFW), TOKENS ** -0.5, 0.09375, ((0, 32), (1, 16)))
    selected = draw_selected(jax.random.fold_in(keys[10], 71), 0)
    owner_keys = jax.random.split(jax.random.fold_in(keys[3], 1), N_TENSOR * PIECES // PIECES)
    owner_turns = jax.random.permutation(jax.random.fold_in(keys[3], 3), N_TENSOR * PIECES // PIECES)
    owner = jax.vmap(lambda own, number: deal_out(jax.random.fold_in(keys[3], 2), own, number, PIECES, N_DP, 1, CAP, 2))(owner_keys, owner_turns).reshape((N_TENSOR, PIECES, 1))
    sel_weight = centred(keys[4], (ROWS, N_TENSOR * SEL_TILES * TILE), 0.5, 3.0, ((0, 32), (1, 16)), jnp.float32)
    sel_moment = centred(keys[5], (ROWS, N_TENSOR * SEL_TILES * TILE), 0.5, 3.0, ((0, 32), (1, 16)), jnp.float32)
    sel_second = jnp.clip(jnp.exp(math.log(1.0) - 4.6051702 * jax.random.uniform(keys[6], (ROWS, N_TENSOR * SEL_TILES * TILE), jnp.float32) ** shard_levels(keys[6], (ROWS, N_TENSOR * SEL_TILES * TILE), ((0, 32), (1, 16)), -0.2, 0.2)), 0.01, 1.0)
    off_weight = centred(keys[7], (N_DP, N_TENSOR, CAP, BLOCK_ROWS, TILE), 0.5, 3.0, ((0, 32), (1, 16)), jnp.float32)
    off_moment = centred(keys[8], (N_DP, N_TENSOR, CAP, BLOCK_ROWS, TILE), 0.5, 3.0, ((0, 32), (1, 16)), jnp.float32)
    off_second = jnp.clip(jnp.exp(math.log(1.0) - 4.6051702 * jax.random.uniform(keys[9], (N_DP, N_TENSOR, CAP, BLOCK_ROWS, TILE), jnp.float32) ** shard_levels(keys[9], (N_DP, N_TENSOR, CAP, BLOCK_ROWS, TILE), ((0, 32), (1, 16)), -0.2, 0.2)), 0.01, 1.0)
    return dict(acts=acts, grad_out=grad_out, selected=selected, owner=owner, sel_weight=sel_weight, sel_moment=sel_moment, sel_second=sel_second, off_weight=off_weight, off_moment=off_moment, off_second=off_second)


beta_one = 0.9
beta_two = 0.95
adam_eps = 1e-08
learn_rate = 0.01
decay_rate = 0.1
step_count = 10.0

def adam_update(weight, moment, second, grad):
    moment_new = beta_one * moment + (1.0 - beta_one) * grad
    second_new = beta_two * second + (1.0 - beta_two) * grad * grad
    first_fix = 1.0 - beta_one ** step_count
    second_fix = 1.0 - beta_two ** step_count
    update = moment_new / first_fix / (jnp.sqrt(second_new / second_fix) + adam_eps)
    return (weight - learn_rate * (update + decay_rate * weight), moment_new, second_new)

def rest_tiles(selected_row):
    tiles = jnp.arange(TILES_DEV, dtype=jnp.int32)
    chosen = jnp.any(tiles[:, None] == selected_row[None, :], axis=1).astype(jnp.int32)
    order = jnp.argsort(chosen * TILES_DEV + tiles).astype(jnp.int32)
    return order[:REST_TILES]

def slot_numbers(owner_row):
    places = jnp.arange(owner_row.shape[0], dtype=jnp.int32)
    earlier = (owner_row[:, None] == owner_row[None, :]) & (places[:, None] > places[None, :])
    return lax.optimization_barrier(jnp.sum(earlier.astype(jnp.int32), axis=1)).astype(jnp.int32)

def place_pieces(piece_row, owner_row):
    target = (owner_row * CAP + slot_numbers(owner_row)).astype(jnp.int32)
    empty = jnp.zeros((N_DP * CAP, BLOCK_ROWS, TILE), jnp.bfloat16)
    return empty.at[target].set(piece_row).reshape(N_DP, CAP, BLOCK_ROWS, TILE)

def reference(acts, grad_out, selected, owner, sel_weight, sel_moment, sel_second, off_weight, off_moment, off_second):
    rest_lists = jax.vmap(rest_tiles)(selected)
    acts_shards = acts.reshape(N_DP, TOK_DEV, ROWS)
    grad_shards = grad_out.reshape(N_DP, TOK_DEV, FFW)
    sel_index = selected.astype(jnp.int32)[None, :, :, None]
    rest_index = rest_lists.astype(jnp.int32)[None, :, :, None]

    def add_shard(carry, shard):
        squares, sel_sum, rest_sum = carry
        partial_value = jnp.dot(shard[0].T, shard[1], preferred_element_type=jnp.float32)
        squares = squares + lax.optimization_barrier(jnp.sum(partial_value * partial_value, axis=0))
        tiled = partial_value.reshape(ROWS, N_TENSOR, TILES_DEV, TILE)
        sel_part = jnp.take_along_axis(tiled, sel_index, axis=2).reshape(ROWS, N_TENSOR * SEL_TILES * TILE)
        rest_part = jnp.take_along_axis(tiled, rest_index, axis=2).astype(jnp.bfloat16)
        rest_part = lax.optimization_barrier(rest_part).astype(jnp.float32)
        return ((squares, sel_sum + sel_part, rest_sum + rest_part), None)
    start = (jnp.zeros((FFW,), jnp.float32), jnp.zeros((ROWS, N_TENSOR * SEL_TILES * TILE), jnp.float32), jnp.zeros((ROWS, N_TENSOR, REST_TILES, TILE), jnp.float32))
    (squares, sel_sum, rest_sum), unused = lax.scan(add_shard, start, (acts_shards, grad_shards))
    column_norm = jnp.sqrt(squares)
    new_sel = adam_update(sel_weight, sel_moment, sel_second, sel_sum)
    pieces = rest_sum.astype(jnp.bfloat16).reshape(N_DP, BLOCK_ROWS, N_TENSOR, REST_TILES, TILE)
    pieces = jnp.transpose(pieces, (2, 3, 0, 1, 4)).reshape(N_TENSOR, PIECES, BLOCK_ROWS, TILE)
    slots = jax.vmap(place_pieces)(pieces, owner[:, :, 0].astype(jnp.int32))
    offload = jnp.transpose(slots, (1, 0, 2, 3, 4)).astype(jnp.float32)
    new_off = adam_update(off_weight, off_moment, off_second, offload)
    return (column_norm, new_sel[0], new_sel[1], new_sel[2], new_off[0], new_off[1], new_off[2])
```

```python
import jax
import jax.numpy as jnp
from jax import lax
from jax.experimental import pallas as pl
from jax.experimental.pallas import tpu as pltpu
from jax.sharding import Mesh
from jax.sharding import PartitionSpec as P

TILE = 128
DP = ("dp_0", "dp_1")


beta_one = 0.9
beta_two = 0.95
adam_eps = 1e-08
learn_rate = 0.01
decay_rate = 0.1
step_count = 10.0


def adam_update(weight, moment, second, grad):
    moment_new = beta_one * moment + (1.0 - beta_one) * grad
    second_new = beta_two * second + (1.0 - beta_two) * grad * grad
    first_fix = 1.0 - beta_one**step_count
    second_fix = 1.0 - beta_two**step_count
    update = moment_new / first_fix / (jnp.sqrt(second_new / second_fix) + adam_eps)
    return (weight - learn_rate * (update + decay_rate * weight), moment_new, second_new)


def slot_numbers(owner_row):
    places = jnp.arange(owner_row.shape[0], dtype=jnp.int32)
    earlier = (owner_row[:, None] == owner_row[None, :]) & (places[:, None] > places[None, :])
    return jnp.sum(earlier.astype(jnp.int32), axis=1)


def replica_sums(
    selected_ref, target_ref, acts_ref, grads_ref, slots_ref, sel_ref, sums, places, *, per_step
):
    step = pl.program_id(0)
    steps = pl.num_programs(0)
    rows, tokens = acts_ref.shape[1:]
    rest_count = sums.shape[0] - 1
    selected = selected_ref[0]

    @pl.when(step == 0)
    def _():
        sums[...] = jnp.zeros_like(sums)

    for k in range(rest_count + 1):
        tile = k + (k >= selected).astype(jnp.int32) if k < rest_count else selected
        column = pl.ds(pl.multiple_of(tile * TILE, TILE), TILE)
        total = sums[k]
        for s in range(per_step):
            partial = jnp.dot(
                acts_ref[s],
                grads_ref[pl.ds(s * tokens, tokens), column],
                preferred_element_type=jnp.float32,
            )
            if k < rest_count:
                partial = partial.astype(jnp.bfloat16).astype(jnp.float32)
            total = total + partial
        sums[k] = total

    @pl.when(step == steps - 1)
    def _():
        blocks, part, _ = sel_ref.shape
        places[...] = jnp.zeros_like(places)
        for k in range(rest_count):
            for b in range(blocks):
                places[target_ref[k * blocks + b]] = sums[k, b * part : (b + 1) * part, :]
        slots_ref[...] = places[...].astype(slots_ref.dtype)
        for b in range(blocks):
            sel_ref[b] = sums[rest_count, b * part : (b + 1) * part, :]


def body(
    acts,
    grad_out,
    selected,
    owner,
    sel_weight,
    sel_moment,
    sel_second,
    off_weight,
    off_moment,
    off_second,
):
    group_size = lax.axis_size(DP)
    tokens_here, rows_all = acts.shape
    cols_here = grad_out.shape[1]
    rest_count = cols_here // TILE - 1
    row_block = rows_all // group_size
    part = row_block // group_size
    capacity = off_weight.shape[2]
    owner_row = owner[0, :, 0]

    strided = acts.T.reshape(group_size, group_size, part, tokens_here)
    strided = jnp.swapaxes(strided, 0, 1).reshape(group_size, row_block, tokens_here)
    acts_rows = lax.all_to_all(strided, DP, split_axis=0, concat_axis=0, tiled=True)
    grads = lax.all_gather(grad_out, DP, axis=0, tiled=True)

    gram = lax.dot_general(acts, acts, (((1,), (1,)), ((), ())), preferred_element_type=jnp.float32)
    grad_wide = grad_out.astype(jnp.float32)
    squares = jnp.sum(grad_wide * jnp.dot(gram, grad_wide, precision=lax.Precision.HIGHEST), axis=0)
    copies = jnp.broadcast_to(squares, (group_size, 1, cols_here))
    squares = lax.all_to_all(copies, DP, split_axis=0, concat_axis=0, tiled=True)
    column_norm = jnp.sqrt(squares.sum(axis=(0, 1)))

    target = owner_row * capacity + slot_numbers(owner_row)
    per_step = 4
    steps = group_size // per_step
    slots, sel_part = pl.pallas_call(
        lambda *refs: replica_sums(*refs, per_step=per_step),
        grid=(steps,),
        in_specs=[
            pl.BlockSpec(memory_space=pltpu.SMEM),
            pl.BlockSpec(memory_space=pltpu.SMEM),
            pl.BlockSpec((per_step, row_block, tokens_here), lambda i: (i, 0, 0)),
            pl.BlockSpec((per_step * tokens_here, cols_here), lambda i: (i, 0)),
        ],
        out_specs=[
            pl.BlockSpec((group_size * capacity, part, TILE), lambda i: (0, 0, 0)),
            pl.BlockSpec((group_size, part, TILE), lambda i: (0, 0, 0)),
        ],
        out_shape=[
            jax.ShapeDtypeStruct((group_size * capacity, part, TILE), jnp.bfloat16),
            jax.ShapeDtypeStruct((group_size, part, TILE), jnp.float32),
        ],
        scratch_shapes=[
            pltpu.VMEM((rest_count + 1, row_block, TILE), jnp.float32),
            pltpu.VMEM((group_size * capacity, part, TILE), jnp.float32),
        ],
        cost_estimate=pl.CostEstimate(
            flops=2 * group_size * tokens_here * row_block * cols_here,
            bytes_accessed=2 * group_size * tokens_here * (row_block + cols_here),
            transcendentals=0,
        ),
        name="replica_sums",
    )(selected[0], target, acts_rows, grads)

    received = lax.all_to_all(
        slots.reshape(group_size, capacity, part, TILE), DP, split_axis=0, concat_axis=0, tiled=True
    )
    sel_sum = lax.all_to_all(sel_part, DP, split_axis=0, concat_axis=0, tiled=True)
    new_sel = adam_update(sel_weight, sel_moment, sel_second, sel_sum.reshape(row_block, TILE))
    offload = jnp.swapaxes(received, 0, 1).reshape(off_weight.shape).astype(jnp.float32)
    new_off = adam_update(off_weight, off_moment, off_second, offload)
    return (column_norm, new_sel[0], new_sel[1], new_sel[2], new_off[0], new_off[1], new_off[2])


def solution(mesh):
    torus = Mesh(mesh.devices.reshape(4, 8, mesh.shape["tensor"]), ("dp_0", "dp_1", "tensor"))
    in_specs = (
        P(DP, None),
        P(DP, "tensor"),
        P("tensor", None),
        P("tensor", None, None),
        P(DP, "tensor"),
        P(DP, "tensor"),
        P(DP, "tensor"),
        P(DP, "tensor", None, None, None),
        P(DP, "tensor", None, None, None),
        P(DP, "tensor", None, None, None),
    )
    out_specs = (
        P("tensor"),
        P(DP, "tensor"),
        P(DP, "tensor"),
        P(DP, "tensor"),
        P(DP, "tensor", None, None, None),
        P(DP, "tensor", None, None, None),
        P(DP, "tensor", None, None, None),
    )
    return jax.shard_map(body, mesh=torus, in_specs=in_specs, out_specs=out_specs, check_vma=False)
```

```python
import jax
import jax.numpy as jnp
from jax import lax
from jax.experimental import pallas as pl
from jax.experimental.pallas import tpu as pltpu
from jax.sharding import Mesh
from jax.sharding import PartitionSpec as P

TILE = 128
EARLY_TILES = 3
DP = ("dp_0", "dp_1")


beta_one = 0.9
beta_two = 0.95
adam_eps = 1e-08
learn_rate = 0.01
decay_rate = 0.1
step_count = 10.0


def adam_update(weight, moment, second, grad):
    moment_new = beta_one * moment + (1.0 - beta_one) * grad
    second_new = beta_two * second + (1.0 - beta_two) * grad * grad
    first_fix = 1.0 - beta_one**step_count
    second_fix = 1.0 - beta_two**step_count
    update = moment_new / first_fix / (jnp.sqrt(second_new / second_fix) + adam_eps)
    return (weight - learn_rate * (update + decay_rate * weight), moment_new, second_new)


def slot_numbers(owner_row):
    places = jnp.arange(owner_row.shape[0], dtype=jnp.int32)
    earlier = (owner_row[:, None] == owner_row[None, :]) & (places[:, None] > places[None, :])
    return jnp.sum(earlier.astype(jnp.int32), axis=1)


def split_three(value):
    high = value.astype(jnp.bfloat16).astype(jnp.float32)
    rest = value - high
    middle = rest.astype(jnp.bfloat16).astype(jnp.float32)
    return high, middle, (rest - middle).astype(jnp.bfloat16).astype(jnp.float32)


def add_replicas(order_ref, selected, mine_ref, other_ref, grads_ref, start, first_tile, sums_ref):
    tokens = mine_ref.shape[2]
    replicas, width = grads_ref.shape[0] // tokens, grads_ref.shape[1]
    unroll = 4
    for low in range(0, width, 2 * TILE):
        wide = min(2 * TILE, width - low)

        def step(j, totals, low=low, wide=wide):
            for u in range(unroll):
                at = j * unroll + u
                source = order_ref[start + at]
                rows = jnp.concatenate([mine_ref[source], other_ref[source]], axis=0)
                place = pl.ds(pl.multiple_of(at * tokens, tokens), tokens)
                partial = jnp.dot(
                    rows, grads_ref[place, low : low + wide], preferred_element_type=jnp.float32
                )
                added = []
                for n, total in enumerate(totals):
                    tile = first_tile + low // TILE + n
                    whole = partial[:, n * TILE : (n + 1) * TILE]
                    rounded = whole.astype(jnp.bfloat16).astype(jnp.float32)
                    added.append(total + jnp.where(selected == tile, whole, rounded))
                totals = tuple(added)
            return totals

        at_tile = low // TILE
        totals = tuple(sums_ref[at_tile + n] for n in range(wide // TILE))
        totals = lax.fori_loop(0, replicas // unroll, step, totals)
        for n, total in enumerate(totals):
            sums_ref[at_tile + n] = total


def chunk_kernel(scalars_ref, mine_ref, other_ref, *refs, starts, first_tile, fresh):
    grads_refs, sums_ref = refs[: len(starts)], refs[-1]
    if fresh:
        sums_ref[...] = jnp.zeros_like(sums_ref)
    else:
        sums_ref[...] = refs[len(starts)][...]
    for grads_ref, start in zip(grads_refs, starts):
        add_replicas(
            scalars_ref, scalars_ref[0], mine_ref, other_ref, grads_ref, start, first_tile, sums_ref
        )


def place_kernel(
    scalars_ref, target_ref, mine_ref, other_ref, *refs, starts, first_tile, owners, slots
):
    grads_refs = refs[: len(starts)]
    early_ref, late_ref, slots_ref, sums, places = refs[len(starts) :]
    selected, flip = scalars_ref[0], scalars_ref[1]
    sums[...] = late_ref[...]
    for grads_ref, start in zip(grads_refs, starts):
        add_replicas(
            scalars_ref, selected, mine_ref, other_ref, grads_ref, start, first_tile, sums
        )
    places[...] = jnp.zeros_like(places)
    part = slots_ref.shape[1]
    for tile in range(first_tile + sums.shape[0]):
        held, at = (early_ref, tile) if tile < first_tile else (sums, tile - first_tile)
        rest = tile - (tile > selected).astype(jnp.int32)

        @pl.when(tile != selected)
        def _(held=held, at=at, rest=rest):
            for q in range(owners):
                places[target_ref[rest * owners + q]] = held[at, q * part : (q + 1) * part, :]

        @pl.when(tile == selected)
        def _(held=held, at=at):
            for q in range(owners):
                owner = jnp.bitwise_xor(q, flip * (owners // 2))
                for n, term in enumerate(split_three(held[at, q * part : (q + 1) * part, :])):
                    places[owner * slots + slots - 3 + n] = term

    slots_ref[...] = places[...].astype(slots_ref.dtype)


def shift(array, axis, by):
    size = lax.axis_size(axis)
    return lax.ppermute(array, axis, [(i, (i + by) % size) for i in range(size)])


def body(
    acts,
    grad_out,
    selected,
    owner,
    sel_weight,
    sel_moment,
    sel_second,
    off_weight,
    off_moment,
    off_second,
):
    group_size = lax.axis_size(DP)
    size_x, size_y = lax.axis_size(DP[0]), lax.axis_size(DP[1])
    at_x, at_y = lax.axis_index(DP[0]), lax.axis_index(DP[1])
    core = lax.rem(lax.axis_index("tensor"), 2)
    tokens_here, rows_all = acts.shape
    cols_here = grad_out.shape[1]
    tiles_here = cols_here // TILE
    early_tiles = EARLY_TILES
    row_block = rows_all // group_size
    part = row_block // group_size
    capacity = off_weight.shape[2]
    slots = capacity + 3
    owner_row = owner[0, :, 0]

    early = lax.all_gather(grad_out[:, : early_tiles * TILE], DP, axis=0, tiled=True)
    late = grad_out[:, early_tiles * TILE :]
    column = jnp.concatenate([late] + [shift(late, DP[1], k) for k in range(1, size_y)], axis=0)
    half = column.shape[0] // 2
    from_left = shift(column, DP[0], 1)
    from_right = shift(column, DP[0], -1)
    far_low = shift(from_left[:half], DP[0], 1)
    far_high = shift(from_right[half:], DP[0], -1)

    half_rows = lax.dynamic_slice_in_dim(acts, core * (rows_all // 2), rows_all // 2, axis=1)
    strided = half_rows.T.reshape(group_size // 2, group_size, part, tokens_here)
    strided = jnp.swapaxes(strided, 0, 1).reshape(group_size, row_block // 2, tokens_here)
    mine = lax.all_to_all(strided, DP, split_axis=0, concat_axis=0, tiled=True)
    other = lax.ppermute(mine, "tensor", [(i, i ^ 1) for i in range(lax.axis_size("tensor"))])

    gram = lax.dot_general(acts, acts, (((1,), (1,)), ((), ())), preferred_element_type=jnp.float32)
    grad_wide = grad_out.astype(jnp.float32)
    squares = jnp.sum(grad_wide * jnp.dot(gram, grad_wide, precision=lax.Precision.HIGHEST), axis=0)
    copies = jnp.broadcast_to(squares, (group_size, 1, cols_here))
    squares = lax.all_to_all(copies, DP, split_axis=0, concat_axis=0, tiled=True)
    column_norm = jnp.sqrt(squares.sum(axis=(0, 1)))

    target = owner_row * slots + slot_numbers(owner_row)
    target = target.reshape(tiles_here - 1, 2, group_size // 2)
    target = jnp.where(core == 0, target, target[:, ::-1]).reshape(-1)
    ys = lax.rem(at_y - jnp.arange(size_y, dtype=jnp.int32) + size_y, size_y)
    xs = [lax.rem(at_x + step + size_x, size_x) for step in (0, -1, 1, 2)]
    order = [jnp.arange(group_size, dtype=jnp.int32)] + [x * size_y + ys for x in xs]
    scalars = jnp.concatenate([jnp.stack([selected[0, 0], core]).astype(jnp.int32)] + order)
    whole = pl.BlockSpec(memory_space=pltpu.VMEM)
    small = pl.BlockSpec(memory_space=pltpu.SMEM)

    def cost(replicas, width):
        return pl.CostEstimate(
            flops=2 * replicas * tokens_here * row_block * width,
            bytes_accessed=2 * replicas * tokens_here * (row_block + width),
            transcendentals=0,
        )

    def chunk(name, grads, start, first_tile, sums=None):
        replicas, width = grads.shape[0] // tokens_here, grads.shape[1]
        extra = [] if sums is None else [sums]
        return pl.pallas_call(
            lambda *refs: chunk_kernel(
                *refs, starts=[start], first_tile=first_tile, fresh=sums is None
            ),
            in_specs=[small] + [whole] * (3 + len(extra)),
            out_specs=whole,
            out_shape=jax.ShapeDtypeStruct((width // TILE, row_block, TILE), jnp.float32),
            cost_estimate=cost(replicas, width),
            compiler_params=pltpu.CompilerParams(vmem_limit_bytes=24 << 20),
            name=name,
        )(scalars, mine, other, grads, *extra)

    early_sums = chunk("early_columns", early, 2, 0)
    base = 2 + group_size
    late_sums = chunk("own_x", column, base, early_tiles)
    late_sums = chunk("left_x", from_left, base + size_y, early_tiles, late_sums)
    late_sums = chunk("right_x", from_right, base + 2 * size_y, early_tiles, late_sums)
    late_tiles = tiles_here - early_tiles
    starts = [base + 3 * size_y, base + 3 * size_y + size_y // 2]
    outgoing = pl.pallas_call(
        lambda *refs: place_kernel(
            *refs, starts=starts, first_tile=early_tiles, owners=group_size, slots=slots
        ),
        in_specs=[small] * 2 + [whole] * 6,
        out_specs=whole,
        out_shape=jax.ShapeDtypeStruct((group_size * slots, part, TILE), jnp.bfloat16),
        scratch_shapes=[
            pltpu.VMEM((late_tiles, row_block, TILE), jnp.float32),
            pltpu.VMEM((group_size * slots, part, TILE), jnp.float32),
        ],
        cost_estimate=cost(size_y, late_tiles * TILE),
        compiler_params=pltpu.CompilerParams(vmem_limit_bytes=24 << 20),
        name="far_x_and_slots",
    )(scalars, target, mine, other, far_low, far_high, early_sums, late_sums)

    received = lax.all_to_all(
        outgoing.reshape(group_size, slots, part, TILE), DP, split_axis=0, concat_axis=0, tiled=True
    ).astype(jnp.float32)
    sel_sum = received[:, capacity] + received[:, capacity + 1] + received[:, capacity + 2]
    new_sel = adam_update(sel_weight, sel_moment, sel_second, sel_sum.reshape(row_block, TILE))
    offload = jnp.swapaxes(received[:, :capacity], 0, 1).reshape(off_weight.shape)
    new_off = adam_update(off_weight, off_moment, off_second, offload)
    return (column_norm, new_sel[0], new_sel[1], new_sel[2], new_off[0], new_off[1], new_off[2])


def solution(mesh):
    torus = Mesh(mesh.devices.reshape(4, 8, mesh.shape["tensor"]), ("dp_0", "dp_1", "tensor"))
    in_specs = (
        P(DP, None),
        P(DP, "tensor"),
        P("tensor", None),
        P("tensor", None, None),
        P(DP, "tensor"),
        P(DP, "tensor"),
        P(DP, "tensor"),
        P(DP, "tensor", None, None, None),
        P(DP, "tensor", None, None, None),
        P(DP, "tensor", None, None, None),
    )
    out_specs = (
        P("tensor"),
        P(DP, "tensor"),
        P(DP, "tensor"),
        P(DP, "tensor"),
        P(DP, "tensor", None, None, None),
        P(DP, "tensor", None, None, None),
        P(DP, "tensor", None, None, None),
    )
    return jax.shard_map(body, mesh=torus, in_specs=in_specs, out_specs=out_specs, check_vma=False)
```

```python
import jax
import jax.numpy as jnp
from jax import lax
from jax.experimental import pallas as pl
from jax.experimental.pallas import tpu as pltpu
from jax.sharding import Mesh
from jax.sharding import PartitionSpec as P

TILE = 128
DP = ("dp_0", "dp_1")


beta_one = 0.9
beta_two = 0.95
adam_eps = 1e-08
learn_rate = 0.01
decay_rate = 0.1
step_count = 10.0


def adam_update(weight, moment, second, grad):
    moment_new = beta_one * moment + (1.0 - beta_one) * grad
    second_new = beta_two * second + (1.0 - beta_two) * grad * grad
    first_fix = 1.0 - beta_one**step_count
    second_fix = 1.0 - beta_two**step_count
    update = moment_new / first_fix / (jnp.sqrt(second_new / second_fix) + adam_eps)
    return (weight - learn_rate * (update + decay_rate * weight), moment_new, second_new)


def slot_numbers(owner_row):
    places = jnp.arange(owner_row.shape[0], dtype=jnp.int32)
    earlier = (owner_row[:, None] == owner_row[None, :]) & (places[:, None] > places[None, :])
    return jnp.sum(earlier.astype(jnp.int32), axis=1)


def split_three(value):
    high = value.astype(jnp.bfloat16).astype(jnp.float32)
    rest = value - high
    middle = rest.astype(jnp.bfloat16).astype(jnp.float32)
    return high, middle, (rest - middle).astype(jnp.bfloat16).astype(jnp.float32)


def lane_groups(array, group, lanes):
    return array[:, group * lanes : (group + 1) * lanes]


def spread_kernel(grads_ref, spread_ref):
    groups, tokens, width = spread_ref.shape
    lanes = TILE // groups
    tiles = grads_ref.shape[1] // TILE
    grads = grads_ref[...]
    padding = [jnp.zeros((tokens, width - tiles * lanes), grads.dtype)]
    for x in range(groups):
        parts = [lane_groups(grads, t * groups + x, lanes) for t in range(tiles)]
        spread_ref[x] = jnp.concatenate(parts + padding, axis=1)


def sums_kernel(scalars_ref, target_ref, grads_ref, *refs, chunks, tiles, owners, slots):
    pairs = [(refs[2 * n], refs[2 * n + 1]) for n in range(len(chunks))]
    slots_ref, sums, places = refs[2 * len(chunks) :]
    selected, flip, at_x = scalars_ref[0], scalars_ref[1], scalars_ref[2]
    groups, group_rows, width = sums.shape
    tokens = pairs[0][0].shape[2]
    lanes = TILE // groups
    lane = lax.broadcasted_iota(jnp.int32, (group_rows, width), 1)
    kept = lane // lanes == selected
    half = group_rows // 2
    for g in range(groups):
        total = jnp.zeros((group_rows, width), jnp.float32)
        for (step_x, first_y), (mine_ref, other_ref) in zip(chunks, pairs):
            x = lax.rem(at_x + step_x, groups)

            def step(j, total, x=x, first_y=first_y, mine_ref=mine_ref, other_ref=other_ref):
                for u in range(4):
                    y = j * 4 + u
                    rows = jnp.concatenate(
                        [ref[y, g * half : (g + 1) * half, :] for ref in (mine_ref, other_ref)],
                        axis=0,
                    )
                    place = ((first_y + y) * groups + x) * tokens
                    partial = jnp.dot(
                        rows,
                        grads_ref[pl.ds(pl.multiple_of(place, tokens), tokens), :],
                        preferred_element_type=jnp.float32,
                    )
                    rounded = partial.astype(jnp.bfloat16).astype(jnp.float32)
                    total = total + jnp.where(kept, partial, rounded)
                return total

            total = lax.fori_loop(0, mine_ref.shape[0] // 4, step, total)
        sums[g] = total

    places[...] = jnp.zeros_like(places)
    part = slots_ref.shape[1]
    for tile in range(tiles):
        rest = tile - (tile > selected).astype(jnp.int32)
        held = jnp.concatenate([lane_groups(sums[g], tile, lanes) for g in range(groups)], axis=1)

        @pl.when(tile != selected)
        def _(held=held, rest=rest):
            for q in range(owners):
                places[target_ref[rest * owners + q]] = held[q * part : (q + 1) * part, :]

        @pl.when(tile == selected)
        def _(held=held):
            for q in range(owners):
                owner = jnp.bitwise_xor(q, flip * (owners // 2))
                for n, term in enumerate(split_three(held[q * part : (q + 1) * part, :])):
                    places[owner * slots + slots - 3 + n] = term

    slots_ref[...] = places[...].astype(slots_ref.dtype)


def owner_kernel(received_ref, *refs, size_x, size_y, part):
    sel_in, off_in, sel_out, off_out = refs[:3], refs[3:6], refs[6:9], refs[9:12]
    grads = refs[12]
    slots = grads.shape[0]
    capacity = slots - 3
    lanes = TILE // size_x
    rows = received_ref.shape[0] // size_x
    sources = [received_ref[pl.ds(x * rows, rows), :].astype(jnp.float32) for x in range(size_x)]
    for g in range(size_x):
        whole = jnp.concatenate([lane_groups(source, g, lanes) for source in sources], axis=1)
        for y in range(size_y):
            for n in range(slots):
                row = (y * slots + n) * part
                place = (y * size_x + g) * part
                grads[n, place : place + part, :] = whole[row : row + part, :]
    sel_sum = grads[capacity] + grads[capacity + 1] + grads[capacity + 2]
    for ref, new in zip(sel_out, adam_update(*(ref[...] for ref in sel_in), sel_sum)):
        ref[...] = new
    for n in range(capacity):
        for ref, new in zip(off_out, adam_update(*(ref[n] for ref in off_in), grads[n])):
            ref[n] = new


def shift(array, axis, by):
    size = lax.axis_size(axis)
    return lax.ppermute(array, axis, [(i, (i + by) % size) for i in range(size)])


def body(
    acts,
    grad_out,
    selected,
    owner,
    sel_weight,
    sel_moment,
    sel_second,
    off_weight,
    off_moment,
    off_second,
):
    group_size = lax.axis_size(DP)
    size_x, size_y = lax.axis_size(DP[0]), lax.axis_size(DP[1])
    at_x = lax.axis_index(DP[0])
    core = lax.rem(lax.axis_index("tensor"), 2)
    tokens_here, rows_all = acts.shape
    cols_here = grad_out.shape[1]
    tiles_here = cols_here // TILE
    row_block = rows_all // group_size
    part = row_block // group_size
    capacity = off_weight.shape[2]
    slots = capacity + 3
    owner_row = owner[0, :, 0]
    width = 2 * TILE
    whole = pl.BlockSpec(memory_space=pltpu.VMEM)
    small = pl.BlockSpec(memory_space=pltpu.SMEM)

    spread = pl.pallas_call(
        spread_kernel,
        in_specs=[whole],
        out_specs=whole,
        out_shape=jax.ShapeDtypeStruct((size_x, tokens_here, width), grad_out.dtype),
        name="spread",
    )(grad_out)
    spread = lax.all_to_all(spread, DP[0], split_axis=0, concat_axis=0, tiled=True)
    grads = lax.all_gather(spread.reshape(size_x * tokens_here, width), DP[1], axis=0, tiled=True)

    halved = lax.dynamic_slice_in_dim(acts, core * (rows_all // 2), rows_all // 2, axis=1)
    halved = halved.T.reshape(group_size // 2, size_y, size_x, part, tokens_here)
    halved = jnp.transpose(halved, (1, 2, 0, 3, 4)).reshape(size_y, -1, tokens_here)
    own = lax.all_to_all(halved, DP[1], split_axis=0, concat_axis=0, tiled=True)
    left, right = shift(own, DP[0], 1), shift(own, DP[0], -1)
    half_y = size_y // 2
    far_low, far_high = shift(left[:half_y], DP[0], 1), shift(right[half_y:], DP[0], -1)
    swap = [(i, i ^ 1) for i in range(lax.axis_size("tensor"))]
    chunks = [(0, 0), (size_x - 1, 0), (1, 0), (2, 0), (2, half_y)]
    acts_rows = []
    for array in (own, left, right, far_low, far_high):
        acts_rows += [array, lax.ppermute(array, "tensor", swap)]

    gram = lax.dot_general(acts, acts, (((1,), (1,)), ((), ())), preferred_element_type=jnp.float32)
    grad_wide = grad_out.astype(jnp.float32)
    squares = jnp.sum(grad_wide * jnp.dot(gram, grad_wide, precision=lax.Precision.HIGHEST), axis=0)
    copies = jnp.broadcast_to(squares, (group_size, 1, cols_here))
    squares = lax.all_to_all(copies, DP, split_axis=0, concat_axis=0, tiled=True)
    column_norm = jnp.sqrt(squares.sum(axis=(0, 1)))

    target = owner_row * slots + slot_numbers(owner_row)
    target = target.reshape(tiles_here - 1, 2, group_size // 2)
    target = jnp.where(core == 0, target, target[:, ::-1]).reshape(-1)
    scalars = jnp.stack([selected[0, 0], core, at_x]).astype(jnp.int32)
    outgoing = pl.pallas_call(
        lambda *refs: sums_kernel(
            *refs, chunks=chunks, tiles=tiles_here, owners=group_size, slots=slots
        ),
        in_specs=[small] * 2 + [whole] * 11,
        out_specs=whole,
        out_shape=jax.ShapeDtypeStruct((group_size * slots, part, TILE), jnp.bfloat16),
        scratch_shapes=[
            pltpu.VMEM((size_x, row_block, width), jnp.float32),
            pltpu.VMEM((group_size * slots, part, TILE), jnp.float32),
        ],
        cost_estimate=pl.CostEstimate(
            flops=2 * group_size * tokens_here * size_x * row_block * width,
            bytes_accessed=2 * group_size * tokens_here * (size_x * row_block + width),
            transcendentals=0,
        ),
        compiler_params=pltpu.CompilerParams(vmem_limit_bytes=32 << 20),
        name="replica_sums",
    )(scalars, target, grads, *acts_rows)

    received = lax.all_to_all(
        outgoing.reshape(group_size, slots * part, TILE), DP, split_axis=0, concat_axis=0, tiled=True
    )
    block = (row_block, TILE)
    outs = pl.pallas_call(
        lambda *refs: owner_kernel(*refs, size_x=size_x, size_y=size_y, part=part),
        in_specs=[whole] * 7,
        out_specs=[whole] * 6,
        out_shape=[jax.ShapeDtypeStruct(block, jnp.float32)] * 3
        + [jax.ShapeDtypeStruct((capacity, *block), jnp.float32)] * 3,
        scratch_shapes=[pltpu.VMEM((slots, *block), jnp.float32)],
        compiler_params=pltpu.CompilerParams(vmem_limit_bytes=24 << 20),
        name="owner_adam",
    )(
        received.reshape(-1, TILE),
        sel_weight,
        sel_moment,
        sel_second,
        *(state.reshape(capacity, *block) for state in (off_weight, off_moment, off_second)),
    )
    return (column_norm, *outs[:3], *(new.reshape(off_weight.shape) for new in outs[3:]))


def solution(mesh):
    torus = Mesh(mesh.devices.reshape(4, 8, mesh.shape["tensor"]), ("dp_0", "dp_1", "tensor"))
    in_specs = (
        P(DP, None),
        P(DP, "tensor"),
        P("tensor", None),
        P("tensor", None, None),
        P(DP, "tensor"),
        P(DP, "tensor"),
        P(DP, "tensor"),
        P(DP, "tensor", None, None, None),
        P(DP, "tensor", None, None, None),
        P(DP, "tensor", None, None, None),
    )
    out_specs = (
        P("tensor"),
        P(DP, "tensor"),
        P(DP, "tensor"),
        P(DP, "tensor"),
        P(DP, "tensor", None, None, None),
        P(DP, "tensor", None, None, None),
        P(DP, "tensor", None, None, None),
    )
    return jax.shard_map(body, mesh=torus, in_specs=in_specs, out_specs=out_specs, check_vma=False)
```

```python
import jax
import jax.numpy as jnp
from jax import lax
from jax.experimental import pallas as pl
from jax.experimental.pallas import tpu as pltpu
from jax.sharding import Mesh
from jax.sharding import PartitionSpec as P

TILE = 128
DP = ("dp_0", "dp_1")


beta_one = 0.9
beta_two = 0.95
adam_eps = 1e-08
learn_rate = 0.01
decay_rate = 0.1
step_count = 10.0


def adam_update(weight, moment, second, grad):
    moment_new = beta_one * moment + (1.0 - beta_one) * grad
    second_new = beta_two * second + (1.0 - beta_two) * grad * grad
    first_fix = 1.0 - beta_one**step_count
    second_fix = 1.0 - beta_two**step_count
    update = moment_new / first_fix / (jnp.sqrt(second_new / second_fix) + adam_eps)
    return (weight - learn_rate * (update + decay_rate * weight), moment_new, second_new)


def slot_numbers(owner_row):
    places = jnp.arange(owner_row.shape[0], dtype=jnp.int32)
    earlier = (owner_row[:, None] == owner_row[None, :]) & (places[:, None] > places[None, :])
    return jnp.sum(earlier.astype(jnp.int32), axis=1)


def split_three(value):
    high = value.astype(jnp.bfloat16).astype(jnp.float32)
    rest = value - high
    middle = rest.astype(jnp.bfloat16).astype(jnp.float32)
    return high, middle, (rest - middle).astype(jnp.bfloat16).astype(jnp.float32)


def lane_groups(array, group, lanes):
    return array[:, group * lanes : (group + 1) * lanes]


def spread_kernel(grads_ref, spread_ref):
    groups, tokens, width = spread_ref.shape
    lanes = TILE // groups
    tiles = grads_ref.shape[1] // TILE
    grads = grads_ref[...]
    padding = [jnp.zeros((tokens, width - tiles * lanes), grads.dtype)]
    for x in range(groups):
        parts = [lane_groups(grads, t * groups + x, lanes) for t in range(tiles)]
        spread_ref[x] = jnp.concatenate(parts + padding, axis=1)


def sums_kernel(scalars_ref, target_ref, grads_ref, *refs, steps_x, tiles, owners, slots):
    pairs = [(refs[2 * n], refs[2 * n + 1]) for n in range(len(steps_x))]
    slots_ref, sums, places = refs[2 * len(steps_x) :]
    selected, flip, at_x = scalars_ref[0], scalars_ref[1], scalars_ref[2]
    groups, group_rows, width = sums.shape
    tokens = pairs[0][0].shape[2]
    lanes = TILE // groups
    half = group_rows // 2

    @pl.when(pl.program_id(0) == 0)
    def _():
        sums[...] = jnp.zeros_like(sums)

    kept = lax.broadcasted_iota(jnp.int32, (group_rows, width), 1) // lanes == selected
    for step_x, pair in zip(steps_x, pairs):
        x = lax.rem(at_x + step_x, groups)
        grads = grads_ref[pl.ds(pl.multiple_of(x * tokens, tokens), tokens), :]
        for g in range(groups):
            rows = [ref[0, g * half : (g + 1) * half, :] for ref in pair]
            partial = jnp.dot(
                jnp.concatenate(rows, axis=0), grads, preferred_element_type=jnp.float32
            )
            rounded = partial.astype(jnp.bfloat16).astype(jnp.float32)
            sums[g] = sums[g] + jnp.where(kept, partial, rounded)

    @pl.when(pl.program_id(0) == pl.num_programs(0) - 1)
    def _():
        place_parts(selected, flip, target_ref, sums, places, slots_ref, tiles, owners, slots)


def place_parts(selected, flip, target_ref, sums, places, slots_ref, tiles, owners, slots):
    groups = sums.shape[0]
    lanes = TILE // groups
    part = slots_ref.shape[1]
    places[...] = jnp.zeros_like(places)
    for tile in range(tiles):
        rest = tile - (tile > selected).astype(jnp.int32)
        held = jnp.concatenate([lane_groups(sums[g], tile, lanes) for g in range(groups)], axis=1)

        @pl.when(tile != selected)
        def _(held=held, rest=rest):
            for q in range(owners):
                places[target_ref[rest * owners + q]] = held[q * part : (q + 1) * part, :]

        @pl.when(tile == selected)
        def _(held=held):
            for q in range(owners):
                owner = jnp.bitwise_xor(q, flip * (owners // 2))
                for n, term in enumerate(split_three(held[q * part : (q + 1) * part, :])):
                    places[owner * slots + slots - 3 + n] = term

    slots_ref[...] = places[...].astype(slots_ref.dtype)


def owner_kernel(received_ref, *refs, size_x, size_y, part):
    states, outs, grads = refs[:6], refs[6:12], refs[12]
    held, new, parts, arrived, sent = refs[13:19], refs[19:25], refs[25], refs[26], refs[27]
    fetch = pltpu.make_async_copy(received_ref, parts, arrived.at[6])
    fetch.start()
    loads = [pltpu.make_async_copy(states[n], held[n], arrived.at[n]) for n in range(6)]
    stores = [pltpu.make_async_copy(new[n], outs[n], sent.at[n]) for n in range(6)]
    for load in loads:
        load.start()
    slots = grads.shape[0]
    capacity = slots - 3
    lanes = TILE // size_x
    rows = received_ref.shape[0] // size_x
    fetch.wait()
    sources = [parts[pl.ds(x * rows, rows), :].astype(jnp.float32) for x in range(size_x)]
    for g in range(size_x):
        whole = jnp.concatenate([lane_groups(source, g, lanes) for source in sources], axis=1)
        for y in range(size_y):
            for n in range(slots):
                row = (y * slots + n) * part
                place = (y * size_x + g) * part
                grads[n, place : place + part, :] = whole[row : row + part, :]
    for load in loads:
        load.wait()
    sel_sum = grads[capacity] + grads[capacity + 1] + grads[capacity + 2]
    for ref, value in zip(new[:3], adam_update(*(ref[...] for ref in held[:3]), sel_sum)):
        ref[...] = value
    for n in range(capacity):
        for ref, value in zip(new[3:], adam_update(*(ref[n] for ref in held[3:]), grads[n])):
            ref[n] = value
    for store in stores:
        store.start()
    for store in stores:
        store.wait()


def shift(array, axis, by):
    size = lax.axis_size(axis)
    return lax.ppermute(array, axis, [(i, (i + by) % size) for i in range(size)])


def body(
    acts,
    grad_out,
    selected,
    owner,
    sel_weight,
    sel_moment,
    sel_second,
    off_weight,
    off_moment,
    off_second,
):
    group_size = lax.axis_size(DP)
    size_x, size_y = lax.axis_size(DP[0]), lax.axis_size(DP[1])
    at_x = lax.axis_index(DP[0])
    core = lax.rem(lax.axis_index("tensor"), 2)
    tokens_here, rows_all = acts.shape
    cols_here = grad_out.shape[1]
    tiles_here = cols_here // TILE
    row_block = rows_all // group_size
    part = row_block // group_size
    capacity = off_weight.shape[2]
    slots = capacity + 3
    owner_row = owner[0, :, 0]
    width = 2 * TILE
    whole = pl.BlockSpec(memory_space=pltpu.VMEM)
    small = pl.BlockSpec(memory_space=pltpu.SMEM)

    spread = pl.pallas_call(
        spread_kernel,
        in_specs=[whole],
        out_specs=whole,
        out_shape=jax.ShapeDtypeStruct((size_x, tokens_here, width), grad_out.dtype),
        name="spread",
    )(grad_out)
    spread = lax.all_to_all(spread, DP[0], split_axis=0, concat_axis=0, tiled=True)
    grads = lax.all_gather(spread.reshape(size_x * tokens_here, width), DP[1], axis=0, tiled=True)

    halved = lax.dynamic_slice_in_dim(acts, core * (rows_all // 2), rows_all // 2, axis=1)
    halved = halved.T.reshape(group_size // 2, size_y, size_x, part, tokens_here)
    halved = jnp.transpose(halved, (1, 2, 0, 3, 4)).reshape(size_y, -1, tokens_here)
    own = lax.all_to_all(halved, DP[1], split_axis=0, concat_axis=0, tiled=True)
    steps_x = [0, size_x - 1, 1, 2]
    swap = [(i, i ^ 1) for i in range(lax.axis_size("tensor"))]
    acts_rows = []
    for array in (own, shift(own, DP[0], 1), shift(own, DP[0], -1), shift(own, DP[0], 2)):
        acts_rows += [array, lax.ppermute(array, "tensor", swap)]

    acts, grad_out, _ = lax.optimization_barrier((acts, grad_out, own))
    gram = lax.dot_general(acts, acts, (((1,), (1,)), ((), ())), preferred_element_type=jnp.float32)
    grad_wide = grad_out.astype(jnp.float32)
    squares = jnp.sum(grad_wide * jnp.dot(gram, grad_wide, precision=lax.Precision.HIGHEST), axis=0)
    copies = jnp.broadcast_to(squares, (group_size, 1, cols_here))
    squares = lax.all_to_all(copies, DP, split_axis=0, concat_axis=0, tiled=True)
    column_norm = jnp.sqrt(squares.sum(axis=(0, 1)))

    target = owner_row * slots + slot_numbers(owner_row)
    target = target.reshape(tiles_here - 1, 2, group_size // 2)
    target = jnp.where(core == 0, target, target[:, ::-1]).reshape(-1)
    scalars = jnp.stack([selected[0, 0], core, at_x]).astype(jnp.int32)
    rows_spec = pl.BlockSpec((1, size_x * row_block // 2, tokens_here), lambda y: (y, 0, 0))
    outgoing = pl.pallas_call(
        lambda *refs: sums_kernel(
            *refs, steps_x=steps_x, tiles=tiles_here, owners=group_size, slots=slots
        ),
        grid=(size_y,),
        in_specs=[small] * 2
        + [pl.BlockSpec((size_x * tokens_here, width), lambda y: (y, 0))]
        + [rows_spec] * len(acts_rows),
        out_specs=pl.BlockSpec((group_size * slots, part, TILE), lambda y: (0, 0, 0)),
        out_shape=jax.ShapeDtypeStruct((group_size * slots, part, TILE), jnp.bfloat16),
        scratch_shapes=[
            pltpu.VMEM((size_x, row_block, width), jnp.float32),
            pltpu.VMEM((group_size * slots, part, TILE), jnp.float32),
        ],
        cost_estimate=pl.CostEstimate(
            flops=2 * group_size * tokens_here * size_x * row_block * width,
            bytes_accessed=2 * group_size * tokens_here * (size_x * row_block + width),
            transcendentals=0,
        ),
        compiler_params=pltpu.CompilerParams(vmem_limit_bytes=56 << 20),
        name="replica_sums",
    )(scalars, target, grads, *acts_rows)

    received = lax.all_to_all(
        outgoing.reshape(group_size, slots * part, TILE), DP, split_axis=0, concat_axis=0, tiled=True
    )
    block = (row_block, TILE)
    states = [block] * 3 + [(capacity, *block)] * 3
    anywhere = pl.BlockSpec(memory_space=pl.ANY)
    outs = pl.pallas_call(
        lambda *refs: owner_kernel(*refs, size_x=size_x, size_y=size_y, part=part),
        in_specs=[anywhere] * 7,
        out_specs=[anywhere] * 6,
        out_shape=[jax.ShapeDtypeStruct(state, jnp.float32) for state in states],
        scratch_shapes=[pltpu.VMEM((slots, *block), jnp.float32)]
        + [pltpu.VMEM(state, jnp.float32) for state in states] * 2
        + [pltpu.VMEM((group_size * slots * part, TILE), jnp.bfloat16)]
        + [pltpu.SemaphoreType.DMA((7,)), pltpu.SemaphoreType.DMA((6,))],
        compiler_params=pltpu.CompilerParams(vmem_limit_bytes=56 << 20),
        name="owner_adam",
    )(
        received.reshape(-1, TILE),
        sel_weight,
        sel_moment,
        sel_second,
        *(state.reshape(capacity, *block) for state in (off_weight, off_moment, off_second)),
    )
    return (column_norm, *outs[:3], *(new.reshape(off_weight.shape) for new in outs[3:]))


def solution(mesh):
    torus = Mesh(mesh.devices.reshape(4, 8, mesh.shape["tensor"]), ("dp_0", "dp_1", "tensor"))
    in_specs = (
        P(DP, None),
        P(DP, "tensor"),
        P("tensor", None),
        P("tensor", None, None),
        P(DP, "tensor"),
        P(DP, "tensor"),
        P(DP, "tensor"),
        P(DP, "tensor", None, None, None),
        P(DP, "tensor", None, None, None),
        P(DP, "tensor", None, None, None),
    )
    out_specs = (
        P("tensor"),
        P(DP, "tensor"),
        P(DP, "tensor"),
        P(DP, "tensor"),
        P(DP, "tensor", None, None, None),
        P(DP, "tensor", None, None, None),
        P(DP, "tensor", None, None, None),
    )
    return jax.shard_map(body, mesh=torus, in_specs=in_specs, out_specs=out_specs, check_vma=False)
```

```python
import jax
import jax.numpy as jnp
from jax import lax
from jax.experimental import pallas as pl
from jax.experimental.pallas import tpu as pltpu
from jax.sharding import Mesh
from jax.sharding import PartitionSpec as P

TILE = 128
DP = ("dp_0", "dp_1")


beta_one = 0.9
beta_two = 0.95
adam_eps = 1e-08
learn_rate = 0.01
decay_rate = 0.1
step_count = 10.0


def adam_update(weight, moment, second, grad):
    moment_new = beta_one * moment + (1.0 - beta_one) * grad
    second_new = beta_two * second + (1.0 - beta_two) * grad * grad
    first_fix = 1.0 - beta_one**step_count
    second_fix = 1.0 - beta_two**step_count
    update = moment_new / first_fix / (jnp.sqrt(second_new / second_fix) + adam_eps)
    return (weight - learn_rate * (update + decay_rate * weight), moment_new, second_new)


def slot_numbers(owner_row):
    places = jnp.arange(owner_row.shape[0], dtype=jnp.int32)
    earlier = (owner_row[:, None] == owner_row[None, :]) & (places[:, None] > places[None, :])
    return jnp.sum(earlier.astype(jnp.int32), axis=1)


def split_three(value):
    high = value.astype(jnp.bfloat16).astype(jnp.float32)
    rest = value - high
    middle = rest.astype(jnp.bfloat16).astype(jnp.float32)
    return high, middle, (rest - middle).astype(jnp.bfloat16).astype(jnp.float32)


def lane_groups(array, group, lanes):
    return array[:, group * lanes : (group + 1) * lanes]


def spread_kernel(grads_ref, spread_ref):
    groups, tokens, width = spread_ref.shape
    lanes = TILE // groups
    tiles = grads_ref.shape[1] // TILE
    grads = grads_ref[...]
    padding = [jnp.zeros((tokens, width - tiles * lanes), grads.dtype)]
    for x in range(groups):
        parts = [lane_groups(grads, t * groups + x, lanes) for t in range(tiles)]
        spread_ref[x] = jnp.concatenate(parts + padding, axis=1)


def sums_kernel(scalars_ref, target_ref, grads_ref, *refs, steps_x, tiles, owners, slots):
    pairs = [(refs[2 * n], refs[2 * n + 1]) for n in range(len(steps_x))]
    slots_ref, sums, squares, places = refs[2 * len(steps_x) :]
    selected, flip, at_x = scalars_ref[0], scalars_ref[1], scalars_ref[2]
    groups, group_rows, width = sums.shape
    tokens = pairs[0][0].shape[2]
    lanes = TILE // groups
    half = group_rows // 2

    @pl.when(pl.program_id(0) == 0)
    def _():
        sums[...] = jnp.zeros_like(sums)
        squares[...] = jnp.zeros_like(squares)

    kept = lax.broadcasted_iota(jnp.int32, (group_rows, width), 1) // lanes == selected
    column_squares = squares[...]
    for g in range(groups):
        total = sums[g]
        for step_x, pair in zip(steps_x, pairs):
            x = lax.rem(at_x + step_x, groups)
            rows = [ref[0, g * half : (g + 1) * half, :] for ref in pair]
            partial = jnp.dot(
                jnp.concatenate(rows, axis=0),
                grads_ref[pl.ds(pl.multiple_of(x * tokens, tokens), tokens), :],
                preferred_element_type=jnp.float32,
            )
            rounded = partial.astype(jnp.bfloat16).astype(jnp.float32)
            total = total + jnp.where(kept, partial, rounded)
            squared = (partial * partial).reshape(-1, *column_squares.shape)
            column_squares = column_squares + squared.sum(axis=0)
        sums[g] = total
    squares[...] = column_squares

    @pl.when(pl.program_id(0) == pl.num_programs(0) - 1)
    def _():
        place_parts(
            selected, flip, target_ref, sums, column_squares, places, slots_ref, tiles, owners, slots
        )


def place_parts(
    selected, flip, target_ref, sums, column_squares, places, slots_ref, tiles, owners, slots
):
    groups = sums.shape[0]
    lanes = TILE // groups
    part = slots_ref.shape[1]
    places[...] = jnp.zeros_like(places)
    for tile in range(tiles):
        rest = tile - (tile > selected).astype(jnp.int32)
        held = jnp.concatenate([lane_groups(sums[g], tile, lanes) for g in range(groups)], axis=1)

        @pl.when(tile != selected)
        def _(held=held, rest=rest):
            for q in range(owners):
                places[target_ref[rest * owners + q]] = held[q * part : (q + 1) * part, :]

        @pl.when(tile == selected)
        def _(held=held):
            for q in range(owners):
                owner = jnp.bitwise_xor(q, flip * (owners // 2))
                for n, term in enumerate(split_three(held[q * part : (q + 1) * part, :])):
                    places[owner * slots + slots - 5 + n] = term

    terms = []
    for term in split_three(jnp.sum(column_squares, axis=0, keepdims=True)):
        terms += [term[:, :TILE], term[:, TILE:]]
    terms += [jnp.zeros_like(terms[0])] * 2
    for n in range(2):
        rows = jnp.concatenate(terms[n * part : (n + 1) * part], axis=0)
        for q in range(owners):
            places[q * slots + slots - 2 + n] = rows

    slots_ref[...] = places[...].astype(slots_ref.dtype)


def owner_kernel(received_ref, *refs, size_x, size_y, part):
    states, outs, norms_ref, grads = refs[:6], refs[6:12], refs[12], refs[13]
    held, new, parts, arrived, sent = refs[14:20], refs[20:26], refs[26], refs[27], refs[28]
    fetch = pltpu.make_async_copy(received_ref, parts, arrived.at[6])
    fetch.start()
    loads = [pltpu.make_async_copy(states[n], held[n], arrived.at[n]) for n in range(6)]
    stores = [pltpu.make_async_copy(new[n], outs[n], sent.at[n]) for n in range(6)]
    for load in loads:
        load.start()
    used = grads.shape[0]
    capacity = used - 3
    slots = used + 2
    lanes = TILE // size_x
    rows = received_ref.shape[0] // size_x
    fetch.wait()
    sources = [parts[pl.ds(x * rows, rows), :].astype(jnp.float32) for x in range(size_x)]
    for g in range(size_x):
        whole = jnp.concatenate([lane_groups(source, g, lanes) for source in sources], axis=1)
        for y in range(size_y):
            for n in range(used):
                row = (y * slots + n) * part
                place = (y * size_x + g) * part
                grads[n, place : place + part, :] = whole[row : row + part, :]
    norms = []
    for source in sources:
        rows = sum(source[(y * slots + used) * part :][: 2 * part] for y in range(size_y))
        norms.append(jnp.sqrt(rows[0:2] + rows[2:4] + rows[4:6]))
    for tile in range(norms_ref.shape[0]):
        row, group = divmod(tile, size_x)
        norms_ref[tile : tile + 1, :] = jnp.concatenate(
            [lane_groups(norm[row : row + 1], group, lanes) for norm in norms], axis=1
        )
    for load in loads:
        load.wait()
    sel_sum = grads[capacity] + grads[capacity + 1] + grads[capacity + 2]
    for ref, value in zip(new[:3], adam_update(*(ref[...] for ref in held[:3]), sel_sum)):
        ref[...] = value
    for n in range(capacity):
        for ref, value in zip(new[3:], adam_update(*(ref[n] for ref in held[3:]), grads[n])):
            ref[n] = value
    for store in stores:
        store.start()
    for store in stores:
        store.wait()


def shift(array, axis, by):
    size = lax.axis_size(axis)
    return lax.ppermute(array, axis, [(i, (i + by) % size) for i in range(size)])


def body(
    acts,
    grad_out,
    selected,
    owner,
    sel_weight,
    sel_moment,
    sel_second,
    off_weight,
    off_moment,
    off_second,
):
    group_size = lax.axis_size(DP)
    size_x, size_y = lax.axis_size(DP[0]), lax.axis_size(DP[1])
    at_x = lax.axis_index(DP[0])
    core = lax.rem(lax.axis_index("tensor"), 2)
    tokens_here, rows_all = acts.shape
    cols_here = grad_out.shape[1]
    tiles_here = cols_here // TILE
    row_block = rows_all // group_size
    part = row_block // group_size
    capacity = off_weight.shape[2]
    slots = capacity + 5
    owner_row = owner[0, :, 0]
    width = 2 * TILE
    whole = pl.BlockSpec(memory_space=pltpu.VMEM)
    small = pl.BlockSpec(memory_space=pltpu.SMEM)

    spread = pl.pallas_call(
        spread_kernel,
        in_specs=[whole],
        out_specs=whole,
        out_shape=jax.ShapeDtypeStruct((size_x, tokens_here, width), grad_out.dtype),
        name="spread",
    )(grad_out)
    spread = lax.all_to_all(spread, DP[0], split_axis=0, concat_axis=0, tiled=True)
    grads = lax.all_gather(spread.reshape(size_x * tokens_here, width), DP[1], axis=0, tiled=True)

    halved = lax.dynamic_slice_in_dim(acts, core * (rows_all // 2), rows_all // 2, axis=1)
    halved = halved.T.reshape(group_size // 2, size_y, size_x, part, tokens_here)
    halved = jnp.transpose(halved, (1, 2, 0, 3, 4)).reshape(size_y, -1, tokens_here)
    own = lax.all_to_all(halved, DP[1], split_axis=0, concat_axis=0, tiled=True)
    steps_x = [0, size_x - 1, 1, 2]
    left = shift(own, DP[0], 1)
    target = owner_row * slots + slot_numbers(owner_row)
    target = target.reshape(tiles_here - 1, 2, group_size // 2)
    target = jnp.where(core == 0, target, target[:, ::-1]).reshape(-1)
    scalars = jnp.stack([selected[0, 0], core, at_x]).astype(jnp.int32)
    left, target, scalars = lax.optimization_barrier((left, target, scalars))
    swap = [(i, i ^ 1) for i in range(lax.axis_size("tensor"))]
    acts_rows = []
    for array in (own, left, shift(own, DP[0], -1), shift(own, DP[0], 2)):
        acts_rows += [array, lax.ppermute(array, "tensor", swap)]
    rows_spec = pl.BlockSpec((1, size_x * row_block // 2, tokens_here), lambda y: (y, 0, 0))
    outgoing = pl.pallas_call(
        lambda *refs: sums_kernel(
            *refs, steps_x=steps_x, tiles=tiles_here, owners=group_size, slots=slots
        ),
        grid=(size_y,),
        in_specs=[small] * 2
        + [pl.BlockSpec((size_x * tokens_here, width), lambda y: (y, 0))]
        + [rows_spec] * len(acts_rows),
        out_specs=pl.BlockSpec((group_size * slots, part, TILE), lambda y: (0, 0, 0)),
        out_shape=jax.ShapeDtypeStruct((group_size * slots, part, TILE), jnp.bfloat16),
        scratch_shapes=[
            pltpu.VMEM((size_x, row_block, width), jnp.float32),
            pltpu.VMEM((8, width), jnp.float32),
            pltpu.VMEM((group_size * slots, part, TILE), jnp.float32),
        ],
        cost_estimate=pl.CostEstimate(
            flops=2 * group_size * tokens_here * size_x * row_block * width,
            bytes_accessed=2 * group_size * tokens_here * (size_x * row_block + width),
            transcendentals=0,
        ),
        compiler_params=pltpu.CompilerParams(vmem_limit_bytes=56 << 20),
        name="replica_sums",
    )(scalars, target, grads, *acts_rows)

    received = lax.all_to_all(
        outgoing.reshape(group_size, slots * part, TILE), DP, split_axis=0, concat_axis=0, tiled=True
    )
    block = (row_block, TILE)
    states = [block] * 3 + [(capacity, *block)] * 3
    anywhere = pl.BlockSpec(memory_space=pl.ANY)
    outs = pl.pallas_call(
        lambda *refs: owner_kernel(*refs, size_x=size_x, size_y=size_y, part=part),
        in_specs=[anywhere] * 7,
        out_specs=[anywhere] * 6 + [whole],
        out_shape=[jax.ShapeDtypeStruct(state, jnp.float32) for state in states]
        + [jax.ShapeDtypeStruct((tiles_here, TILE), jnp.float32)],
        scratch_shapes=[pltpu.VMEM((capacity + 3, *block), jnp.float32)]
        + [pltpu.VMEM(state, jnp.float32) for state in states] * 2
        + [pltpu.VMEM((group_size * slots * part, TILE), jnp.bfloat16)]
        + [pltpu.SemaphoreType.DMA((7,)), pltpu.SemaphoreType.DMA((6,))],
        compiler_params=pltpu.CompilerParams(vmem_limit_bytes=56 << 20),
        name="owner_adam",
    )(
        received.reshape(-1, TILE),
        sel_weight,
        sel_moment,
        sel_second,
        *(state.reshape(capacity, *block) for state in (off_weight, off_moment, off_second)),
    )
    off_new = [new.reshape(off_weight.shape) for new in outs[3:6]]
    return (outs[6].reshape(-1), *outs[:3], *off_new)


def solution(mesh):
    torus = Mesh(mesh.devices.reshape(4, 8, mesh.shape["tensor"]), ("dp_0", "dp_1", "tensor"))
    in_specs = (
        P(DP, None),
        P(DP, "tensor"),
        P("tensor", None),
        P("tensor", None, None),
        P(DP, "tensor"),
        P(DP, "tensor"),
        P(DP, "tensor"),
        P(DP, "tensor", None, None, None),
        P(DP, "tensor", None, None, None),
        P(DP, "tensor", None, None, None),
    )
    out_specs = (
        P("tensor"),
        P(DP, "tensor"),
        P(DP, "tensor"),
        P(DP, "tensor"),
        P(DP, "tensor", None, None, None),
        P(DP, "tensor", None, None, None),
        P(DP, "tensor", None, None, None),
    )
    return jax.shard_map(body, mesh=torus, in_specs=in_specs, out_specs=out_specs, check_vma=False)
```

```python
import jax
import jax.numpy as jnp
from jax import lax
from jax.experimental import pallas as pl
from jax.experimental.pallas import tpu as pltpu
from jax.sharding import Mesh
from jax.sharding import PartitionSpec as P

TILE = 128
DP = ("dp_0", "dp_1")


beta_one = 0.9
beta_two = 0.95
adam_eps = 1e-08
learn_rate = 0.01
decay_rate = 0.1
step_count = 10.0


def adam_update(weight, moment, second, grad):
    moment_new = beta_one * moment + (1.0 - beta_one) * grad
    second_new = beta_two * second + (1.0 - beta_two) * grad * grad
    first_fix = 1.0 - beta_one**step_count
    second_fix = 1.0 - beta_two**step_count
    update = moment_new / first_fix / (jnp.sqrt(second_new / second_fix) + adam_eps)
    return (weight - learn_rate * (update + decay_rate * weight), moment_new, second_new)


def slot_numbers(owner_row):
    places = jnp.arange(owner_row.shape[0], dtype=jnp.int32)
    earlier = (owner_row[:, None] == owner_row[None, :]) & (places[:, None] > places[None, :])
    return jnp.sum(earlier.astype(jnp.int32), axis=1)


def split_three(value):
    high = value.astype(jnp.bfloat16).astype(jnp.float32)
    rest = value - high
    middle = rest.astype(jnp.bfloat16).astype(jnp.float32)
    return high, middle, (rest - middle).astype(jnp.bfloat16).astype(jnp.float32)


def lane_groups(array, group, lanes):
    return array[:, group * lanes : (group + 1) * lanes]


def spread_kernel(grads_ref, spread_ref):
    groups, tokens, width = spread_ref.shape
    lanes = TILE // groups
    tiles = grads_ref.shape[1] // TILE
    grads = grads_ref[...]
    padding = [jnp.zeros((tokens, width - tiles * lanes), grads.dtype)]
    for x in range(groups):
        parts = [lane_groups(grads, t * groups + x, lanes) for t in range(tiles)]
        spread_ref[x] = jnp.concatenate(parts + padding, axis=1)


def sums_kernel(scalars_ref, target_ref, grads_ref, *refs, steps_x, tiles, owners, slots):
    pairs = [(refs[2 * n], refs[2 * n + 1]) for n in range(len(steps_x))]
    slots_ref, sums, squares, places = refs[2 * len(steps_x) :]
    selected, flip, at_x = scalars_ref[0], scalars_ref[1], scalars_ref[2]
    groups, group_rows, width = sums.shape
    tokens = pairs[0][0].shape[2]
    lanes = TILE // groups
    half = group_rows // 2

    @pl.when(pl.program_id(0) == 0)
    def _():
        sums[...] = jnp.zeros_like(sums)
        squares[...] = jnp.zeros_like(squares)

    kept = lax.broadcasted_iota(jnp.int32, (group_rows, width), 1) // lanes == selected
    column_squares = squares[...]
    for g in range(groups):
        total = sums[g]
        for step_x, pair in zip(steps_x, pairs):
            x = lax.rem(at_x + step_x, groups)
            rows = [ref[0, g * half : (g + 1) * half, :] for ref in pair]
            partial = jnp.dot(
                jnp.concatenate(rows, axis=0),
                grads_ref[pl.ds(pl.multiple_of(x * tokens, tokens), tokens), :],
                preferred_element_type=jnp.float32,
            )
            rounded = partial.astype(jnp.bfloat16).astype(jnp.float32)
            total = total + jnp.where(kept, partial, rounded)
            squared = (partial * partial).reshape(-1, *column_squares.shape)
            column_squares = column_squares + squared.sum(axis=0)
        sums[g] = total
    squares[...] = column_squares

    @pl.when(pl.program_id(0) == pl.num_programs(0) - 1)
    def _():
        place_parts(
            selected, flip, target_ref, sums, column_squares, places, slots_ref, tiles, owners, slots
        )


def place_parts(
    selected, flip, target_ref, sums, column_squares, places, slots_ref, tiles, owners, slots
):
    groups = sums.shape[0]
    lanes = TILE // groups
    part = slots_ref.shape[1]
    places[...] = jnp.zeros_like(places)
    for tile in range(tiles):
        rest = tile - (tile > selected).astype(jnp.int32)
        held = jnp.concatenate([lane_groups(sums[g], tile, lanes) for g in range(groups)], axis=1)

        @pl.when(tile != selected)
        def _(held=held, rest=rest):
            for q in range(owners):
                places[target_ref[rest * owners + q]] = held[q * part : (q + 1) * part, :]

        @pl.when(tile == selected)
        def _(held=held):
            for q in range(owners):
                owner = jnp.bitwise_xor(q, flip * (owners // 2))
                for n, term in enumerate(split_three(held[q * part : (q + 1) * part, :])):
                    places[owner * slots + slots - 5 + n] = term

    terms = []
    for term in split_three(jnp.sum(column_squares, axis=0, keepdims=True)):
        terms += [term[:, :TILE], term[:, TILE:]]
    terms += [jnp.zeros_like(terms[0])] * 2
    for n in range(2):
        rows = jnp.concatenate(terms[n * part : (n + 1) * part], axis=0)
        for q in range(owners):
            places[q * slots + slots - 2 + n] = rows

    slots_ref[...] = places[...].astype(slots_ref.dtype)


def owner_kernel(received_ref, *refs, size_x, size_y, part):
    states, outs, norms_ref, grads = refs[:6], refs[6:12], refs[12], refs[13]
    held, new, parts, arrived, sent = refs[14:20], refs[20:26], refs[26], refs[27], refs[28]
    fetch = pltpu.make_async_copy(received_ref, parts, arrived.at[6])
    fetch.start()
    loads = [pltpu.make_async_copy(states[n], held[n], arrived.at[n]) for n in range(6)]
    stores = [pltpu.make_async_copy(new[n], outs[n], sent.at[n]) for n in range(6)]
    for load in loads:
        load.start()
    used = grads.shape[0]
    capacity = used - 3
    slots = used + 2
    lanes = TILE // size_x
    rows = received_ref.shape[0] // size_x
    fetch.wait()
    sources = [parts[pl.ds(x * rows, rows), :].astype(jnp.float32) for x in range(size_x)]
    for g in range(size_x):
        whole = jnp.concatenate([lane_groups(source, g, lanes) for source in sources], axis=1)
        for y in range(size_y):
            for n in range(used):
                row = (y * slots + n) * part
                place = (y * size_x + g) * part
                grads[n, place : place + part, :] = whole[row : row + part, :]
    norms = []
    for source in sources:
        rows = sum(source[(y * slots + used) * part :][: 2 * part] for y in range(size_y))
        norms.append(jnp.sqrt(rows[0:2] + rows[2:4] + rows[4:6]))
    for tile in range(norms_ref.shape[0]):
        row, group = divmod(tile, size_x)
        norms_ref[tile : tile + 1, :] = jnp.concatenate(
            [lane_groups(norm[row : row + 1], group, lanes) for norm in norms], axis=1
        )
    for load in loads:
        load.wait()
    sel_sum = grads[capacity] + grads[capacity + 1] + grads[capacity + 2]
    for ref, value in zip(new[:3], adam_update(*(ref[...] for ref in held[:3]), sel_sum)):
        ref[...] = value
    for n in range(capacity):
        for ref, value in zip(new[3:], adam_update(*(ref[n] for ref in held[3:]), grads[n])):
            ref[n] = value
    for store in stores:
        store.start()
    for store in stores:
        store.wait()


def shift(array, axis, by):
    size = lax.axis_size(axis)
    return lax.ppermute(array, axis, [(i, (i + by) % size) for i in range(size)])


def body(
    acts,
    grad_out,
    selected,
    owner,
    sel_weight,
    sel_moment,
    sel_second,
    off_weight,
    off_moment,
    off_second,
):
    group_size = lax.axis_size(DP)
    size_x, size_y = lax.axis_size(DP[0]), lax.axis_size(DP[1])
    at_x = lax.axis_index(DP[0])
    core = lax.rem(lax.axis_index("tensor"), 2)
    tokens_here, rows_all = acts.shape
    cols_here = grad_out.shape[1]
    tiles_here = cols_here // TILE
    row_block = rows_all // group_size
    part = row_block // group_size
    capacity = off_weight.shape[2]
    slots = capacity + 5
    owner_row = owner[0, :, 0]
    width = 2 * TILE
    whole = pl.BlockSpec(memory_space=pltpu.VMEM)
    small = pl.BlockSpec(memory_space=pltpu.SMEM)

    spread = pl.pallas_call(
        spread_kernel,
        in_specs=[whole],
        out_specs=whole,
        out_shape=jax.ShapeDtypeStruct((size_x, tokens_here, width), grad_out.dtype),
        name="spread",
    )(grad_out)
    spread = lax.all_to_all(spread, DP[0], split_axis=0, concat_axis=0, tiled=True)
    grads = lax.all_gather(spread.reshape(size_x * tokens_here, width), DP[1], axis=0, tiled=True)

    halved = lax.dynamic_slice_in_dim(acts, core * (rows_all // 2), rows_all // 2, axis=1)
    halved = halved.T.reshape(group_size // 2, size_y, size_x, part, tokens_here)
    halved = jnp.transpose(halved, (1, 2, 0, 3, 4)).reshape(size_y, -1, tokens_here)
    own = lax.all_to_all(halved, DP[1], split_axis=0, concat_axis=0, tiled=True)
    steps_x = [0, size_x - 1, 1, 2]
    left, right = shift(own, DP[0], 1), shift(own, DP[0], -1)
    target = owner_row * slots + slot_numbers(owner_row)
    target = target.reshape(tiles_here - 1, 2, group_size // 2)
    target = jnp.where(core == 0, target, target[:, ::-1]).reshape(-1)
    scalars = jnp.stack([selected[0, 0], core, at_x]).astype(jnp.int32)
    left, target, scalars = lax.optimization_barrier((left, target, scalars))
    swap = [(i, i ^ 1) for i in range(lax.axis_size("tensor"))]
    acts_rows = []
    for array in (own, left, right, shift(right, DP[0], -1)):
        acts_rows += [array, lax.ppermute(array, "tensor", swap)]
    rows_spec = pl.BlockSpec((1, size_x * row_block // 2, tokens_here), lambda y: (y, 0, 0))
    outgoing = pl.pallas_call(
        lambda *refs: sums_kernel(
            *refs, steps_x=steps_x, tiles=tiles_here, owners=group_size, slots=slots
        ),
        grid=(size_y,),
        in_specs=[small] * 2
        + [pl.BlockSpec((size_x * tokens_here, width), lambda y: (y, 0))]
        + [rows_spec] * len(acts_rows),
        out_specs=pl.BlockSpec((group_size * slots, part, TILE), lambda y: (0, 0, 0)),
        out_shape=jax.ShapeDtypeStruct((group_size * slots, part, TILE), jnp.bfloat16),
        scratch_shapes=[
            pltpu.VMEM((size_x, row_block, width), jnp.float32),
            pltpu.VMEM((8, width), jnp.float32),
            pltpu.VMEM((group_size * slots, part, TILE), jnp.float32),
        ],
        cost_estimate=pl.CostEstimate(
            flops=2 * group_size * tokens_here * size_x * row_block * width,
            bytes_accessed=2 * group_size * tokens_here * (size_x * row_block + width),
            transcendentals=0,
        ),
        compiler_params=pltpu.CompilerParams(vmem_limit_bytes=56 << 20),
        name="replica_sums",
    )(scalars, target, grads, *acts_rows)

    received = lax.all_to_all(
        outgoing.reshape(group_size, slots * part, TILE), DP, split_axis=0, concat_axis=0, tiled=True
    )
    block = (row_block, TILE)
    states = [block] * 3 + [(capacity, *block)] * 3
    anywhere = pl.BlockSpec(memory_space=pl.ANY)
    outs = pl.pallas_call(
        lambda *refs: owner_kernel(*refs, size_x=size_x, size_y=size_y, part=part),
        in_specs=[anywhere] * 7,
        out_specs=[anywhere] * 6 + [whole],
        out_shape=[jax.ShapeDtypeStruct(state, jnp.float32) for state in states]
        + [jax.ShapeDtypeStruct((tiles_here, TILE), jnp.float32)],
        scratch_shapes=[pltpu.VMEM((capacity + 3, *block), jnp.float32)]
        + [pltpu.VMEM(state, jnp.float32) for state in states] * 2
        + [pltpu.VMEM((group_size * slots * part, TILE), jnp.bfloat16)]
        + [pltpu.SemaphoreType.DMA((7,)), pltpu.SemaphoreType.DMA((6,))],
        compiler_params=pltpu.CompilerParams(vmem_limit_bytes=56 << 20),
        name="owner_adam",
    )(
        received.reshape(-1, TILE),
        sel_weight,
        sel_moment,
        sel_second,
        *(state.reshape(capacity, *block) for state in (off_weight, off_moment, off_second)),
    )
    off_new = [new.reshape(off_weight.shape) for new in outs[3:6]]
    return (outs[6].reshape(-1), *outs[:3], *off_new)


def solution(mesh):
    torus = Mesh(mesh.devices.reshape(4, 8, mesh.shape["tensor"]), ("dp_0", "dp_1", "tensor"))
    in_specs = (
        P(DP, None),
        P(DP, "tensor"),
        P("tensor", None),
        P("tensor", None, None),
        P(DP, "tensor"),
        P(DP, "tensor"),
        P(DP, "tensor"),
        P(DP, "tensor", None, None, None),
        P(DP, "tensor", None, None, None),
        P(DP, "tensor", None, None, None),
    )
    out_specs = (
        P("tensor"),
        P(DP, "tensor"),
        P(DP, "tensor"),
        P(DP, "tensor"),
        P(DP, "tensor", None, None, None),
        P(DP, "tensor", None, None, None),
        P(DP, "tensor", None, None, None),
    )
    return jax.shard_map(body, mesh=torus, in_specs=in_specs, out_specs=out_specs, check_vma=False)
```

```python
import jax
import jax.numpy as jnp
from jax import lax
from jax.experimental import pallas as pl
from jax.experimental.pallas import tpu as pltpu
from jax.sharding import Mesh
from jax.sharding import PartitionSpec as P

TILE = 128
DP = ("dp_0", "dp_1")


beta_one = 0.9
beta_two = 0.95
adam_eps = 1e-08
learn_rate = 0.01
decay_rate = 0.1
step_count = 10.0


def adam_update(weight, moment, second, grad):
    moment_new = beta_one * moment + (1.0 - beta_one) * grad
    second_new = beta_two * second + (1.0 - beta_two) * grad * grad
    first_fix = 1.0 - beta_one**step_count
    second_fix = 1.0 - beta_two**step_count
    update = moment_new / first_fix / (jnp.sqrt(second_new / second_fix) + adam_eps)
    return (weight - learn_rate * (update + decay_rate * weight), moment_new, second_new)


def slot_numbers(owner_row):
    places = jnp.arange(owner_row.shape[0], dtype=jnp.int32)
    earlier = (owner_row[:, None] == owner_row[None, :]) & (places[:, None] > places[None, :])
    return jnp.sum(earlier.astype(jnp.int32), axis=1)


def split_three(value):
    high = value.astype(jnp.bfloat16).astype(jnp.float32)
    rest = value - high
    middle = rest.astype(jnp.bfloat16).astype(jnp.float32)
    return high, middle, (rest - middle).astype(jnp.bfloat16).astype(jnp.float32)


def lane_groups(array, group, lanes):
    return array[:, group * lanes : (group + 1) * lanes]


def spread_kernel(grads_ref, spread_ref):
    groups, tokens, width = spread_ref.shape
    lanes = TILE // groups
    tiles = grads_ref.shape[1] // TILE
    grads = grads_ref[...]
    padding = [jnp.zeros((tokens, width - tiles * lanes), grads.dtype)]
    for x in range(groups):
        parts = [lane_groups(grads, t * groups + x, lanes) for t in range(tiles)]
        spread_ref[x] = jnp.concatenate(parts + padding, axis=1)


def sums_kernel(scalars_ref, target_ref, grads_ref, *refs, steps_x, tiles, owners, slots):
    pairs = [(refs[2 * n], refs[2 * n + 1]) for n in range(len(steps_x))]
    slots_ref, sums, squares, places = refs[2 * len(steps_x) :]
    selected, flip, at_x = scalars_ref[0], scalars_ref[1], scalars_ref[2]
    groups, group_rows, width = sums.shape
    tokens = pairs[0][0].shape[2]
    lanes = TILE // groups
    half = group_rows // 2

    @pl.when(pl.program_id(0) == 0)
    def _():
        sums[...] = jnp.zeros_like(sums)
        squares[...] = jnp.zeros_like(squares)

    kept = lax.broadcasted_iota(jnp.int32, (group_rows, width), 1) // lanes == selected
    column_squares = squares[...]
    for y in range(pairs[0][0].shape[0]):
        for step_x, pair in zip(steps_x, pairs):
            x = lax.rem(at_x + step_x, groups)
            here = pl.ds(pl.multiple_of((y * groups + x) * tokens, tokens), tokens)
            for g in range(groups):
                rows = [ref[y, g * half : (g + 1) * half, :] for ref in pair]
                partial = jnp.dot(
                    jnp.concatenate(rows, axis=0),
                    grads_ref[here, :],
                    preferred_element_type=jnp.float32,
                )
                rounded = partial.astype(jnp.bfloat16).astype(jnp.float32)
                sums[g] = sums[g] + jnp.where(kept, partial, rounded)
                squared = (partial * partial).reshape(-1, *column_squares.shape)
                column_squares = column_squares + squared.sum(axis=0)
    squares[...] = column_squares

    @pl.when(pl.program_id(0) == pl.num_programs(0) - 1)
    def _():
        place_parts(
            selected, flip, target_ref, sums, column_squares, places, slots_ref, tiles, owners, slots
        )


def place_parts(
    selected, flip, target_ref, sums, column_squares, places, slots_ref, tiles, owners, slots
):
    groups = sums.shape[0]
    lanes = TILE // groups
    part = slots_ref.shape[1]
    places[...] = jnp.zeros_like(places)
    for tile in range(tiles):
        rest = tile - (tile > selected).astype(jnp.int32)
        held = jnp.concatenate([lane_groups(sums[g], tile, lanes) for g in range(groups)], axis=1)

        @pl.when(tile != selected)
        def _(held=held, rest=rest):
            for q in range(owners):
                places[target_ref[rest * owners + q]] = held[q * part : (q + 1) * part, :]

        @pl.when(tile == selected)
        def _(held=held):
            for q in range(owners):
                owner = jnp.bitwise_xor(q, flip * (owners // 2))
                for n, term in enumerate(split_three(held[q * part : (q + 1) * part, :])):
                    places[owner * slots + slots - 5 + n] = term

    terms = []
    for term in split_three(jnp.sum(column_squares, axis=0, keepdims=True)):
        terms += [term[:, :TILE], term[:, TILE:]]
    terms += [jnp.zeros_like(terms[0])] * 2
    for n in range(2):
        rows = jnp.concatenate(terms[n * part : (n + 1) * part], axis=0)
        for q in range(owners):
            places[q * slots + slots - 2 + n] = rows

    slots_ref[...] = places[...].astype(slots_ref.dtype)


def owner_kernel(received_ref, *refs, size_x, size_y, part):
    states, outs, norms_ref, grads = refs[:6], refs[6:12], refs[12], refs[13]
    held, new, parts, arrived, sent = refs[14:20], refs[20:26], refs[26], refs[27], refs[28]
    fetch = pltpu.make_async_copy(received_ref, parts, arrived.at[6])
    fetch.start()
    loads = [pltpu.make_async_copy(states[n], held[n], arrived.at[n]) for n in range(6)]
    stores = [pltpu.make_async_copy(new[n], outs[n], sent.at[n]) for n in range(6)]
    for load in loads:
        load.start()
    used = grads.shape[0]
    capacity = used - 3
    slots = used + 2
    lanes = TILE // size_x
    rows = received_ref.shape[0] // size_x
    fetch.wait()
    sources = [parts[pl.ds(x * rows, rows), :].astype(jnp.float32) for x in range(size_x)]
    for g in range(size_x):
        whole = jnp.concatenate([lane_groups(source, g, lanes) for source in sources], axis=1)
        for y in range(size_y):
            for n in range(used):
                row = (y * slots + n) * part
                place = (y * size_x + g) * part
                grads[n, place : place + part, :] = whole[row : row + part, :]
    norms = []
    for source in sources:
        rows = sum(source[(y * slots + used) * part :][: 2 * part] for y in range(size_y))
        norms.append(jnp.sqrt(rows[0:2] + rows[2:4] + rows[4:6]))
    for tile in range(norms_ref.shape[0]):
        row, group = divmod(tile, size_x)
        norms_ref[tile : tile + 1, :] = jnp.concatenate(
            [lane_groups(norm[row : row + 1], group, lanes) for norm in norms], axis=1
        )
    for load in loads:
        load.wait()
    sel_sum = grads[capacity] + grads[capacity + 1] + grads[capacity + 2]
    for ref, value in zip(new[:3], adam_update(*(ref[...] for ref in held[:3]), sel_sum)):
        ref[...] = value
    for n in range(capacity):
        for ref, value in zip(new[3:], adam_update(*(ref[n] for ref in held[3:]), grads[n])):
            ref[n] = value
    for store in stores:
        store.start()
    for store in stores:
        store.wait()


def shift(array, axis, by):
    size = lax.axis_size(axis)
    return lax.ppermute(array, axis, [(i, (i + by) % size) for i in range(size)])


def body(
    acts,
    grad_out,
    selected,
    owner,
    sel_weight,
    sel_moment,
    sel_second,
    off_weight,
    off_moment,
    off_second,
):
    group_size = lax.axis_size(DP)
    size_x, size_y = lax.axis_size(DP[0]), lax.axis_size(DP[1])
    at_x = lax.axis_index(DP[0])
    core = lax.rem(lax.axis_index("tensor"), 2)
    tokens_here, rows_all = acts.shape
    cols_here = grad_out.shape[1]
    tiles_here = cols_here // TILE
    row_block = rows_all // group_size
    part = row_block // group_size
    capacity = off_weight.shape[2]
    slots = capacity + 5
    owner_row = owner[0, :, 0]
    width = 2 * TILE
    whole = pl.BlockSpec(memory_space=pltpu.VMEM)
    small = pl.BlockSpec(memory_space=pltpu.SMEM)

    spread = pl.pallas_call(
        spread_kernel,
        in_specs=[whole],
        out_specs=whole,
        out_shape=jax.ShapeDtypeStruct((size_x, tokens_here, width), grad_out.dtype),
        name="spread",
    )(grad_out)
    spread = lax.all_to_all(spread, DP[0], split_axis=0, concat_axis=0, tiled=True)
    grads = lax.all_gather(spread.reshape(size_x * tokens_here, width), DP[1], axis=0, tiled=True)

    halved = lax.dynamic_slice_in_dim(acts, core * (rows_all // 2), rows_all // 2, axis=1)
    halved = halved.T.reshape(group_size // 2, size_y, size_x, part, tokens_here)
    halved = jnp.transpose(halved, (1, 2, 0, 3, 4)).reshape(size_y, -1, tokens_here)
    own = lax.all_to_all(halved, DP[1], split_axis=0, concat_axis=0, tiled=True)
    steps_x = [0, size_x - 1, 1, 2]
    left, right = shift(own, DP[0], 1), shift(own, DP[0], -1)
    target = owner_row * slots + slot_numbers(owner_row)
    target = target.reshape(tiles_here - 1, 2, group_size // 2)
    target = jnp.where(core == 0, target, target[:, ::-1]).reshape(-1)
    scalars = jnp.stack([selected[0, 0], core, at_x]).astype(jnp.int32)
    left, target, scalars = lax.optimization_barrier((left, target, scalars))
    swap = [(i, i ^ 1) for i in range(lax.axis_size("tensor"))]
    acts_rows = []
    for array in (own, left, right, shift(right, DP[0], -1)):
        acts_rows += [array, lax.ppermute(array, "tensor", swap)]
    block_y = size_y // 2
    rows_spec = pl.BlockSpec((block_y, size_x * row_block // 2, tokens_here), lambda y: (y, 0, 0))
    outgoing = pl.pallas_call(
        lambda *refs: sums_kernel(
            *refs, steps_x=steps_x, tiles=tiles_here, owners=group_size, slots=slots
        ),
        grid=(size_y // block_y,),
        in_specs=[small] * 2
        + [pl.BlockSpec((block_y * size_x * tokens_here, width), lambda y: (y, 0))]
        + [rows_spec] * len(acts_rows),
        out_specs=pl.BlockSpec((group_size * slots, part, TILE), lambda y: (0, 0, 0)),
        out_shape=jax.ShapeDtypeStruct((group_size * slots, part, TILE), jnp.bfloat16),
        scratch_shapes=[
            pltpu.VMEM((size_x, row_block, width), jnp.float32),
            pltpu.VMEM((8, width), jnp.float32),
            pltpu.VMEM((group_size * slots, part, TILE), jnp.float32),
        ],
        cost_estimate=pl.CostEstimate(
            flops=2 * group_size * tokens_here * size_x * row_block * width,
            bytes_accessed=2 * group_size * tokens_here * (size_x * row_block + width),
            transcendentals=0,
        ),
        compiler_params=pltpu.CompilerParams(vmem_limit_bytes=56 << 20),
        name="replica_sums",
    )(scalars, target, grads, *acts_rows)

    received = lax.all_to_all(
        outgoing.reshape(group_size, slots * part, TILE), DP, split_axis=0, concat_axis=0, tiled=True
    )
    block = (row_block, TILE)
    states = [block] * 3 + [(capacity, *block)] * 3
    anywhere = pl.BlockSpec(memory_space=pl.ANY)
    outs = pl.pallas_call(
        lambda *refs: owner_kernel(*refs, size_x=size_x, size_y=size_y, part=part),
        in_specs=[anywhere] * 7,
        out_specs=[anywhere] * 6 + [whole],
        out_shape=[jax.ShapeDtypeStruct(state, jnp.float32) for state in states]
        + [jax.ShapeDtypeStruct((tiles_here, TILE), jnp.float32)],
        scratch_shapes=[pltpu.VMEM((capacity + 3, *block), jnp.float32)]
        + [pltpu.VMEM(state, jnp.float32) for state in states] * 2
        + [pltpu.VMEM((group_size * slots * part, TILE), jnp.bfloat16)]
        + [pltpu.SemaphoreType.DMA((7,)), pltpu.SemaphoreType.DMA((6,))],
        compiler_params=pltpu.CompilerParams(vmem_limit_bytes=56 << 20),
        name="owner_adam",
    )(
        received.reshape(-1, TILE),
        sel_weight,
        sel_moment,
        sel_second,
        *(state.reshape(capacity, *block) for state in (off_weight, off_moment, off_second)),
    )
    off_new = [new.reshape(off_weight.shape) for new in outs[3:6]]
    return (outs[6].reshape(-1), *outs[:3], *off_new)


def solution(mesh):
    torus = Mesh(mesh.devices.reshape(4, 8, mesh.shape["tensor"]), ("dp_0", "dp_1", "tensor"))
    in_specs = (
        P(DP, None),
        P(DP, "tensor"),
        P("tensor", None),
        P("tensor", None, None),
        P(DP, "tensor"),
        P(DP, "tensor"),
        P(DP, "tensor"),
        P(DP, "tensor", None, None, None),
        P(DP, "tensor", None, None, None),
        P(DP, "tensor", None, None, None),
    )
    out_specs = (
        P("tensor"),
        P(DP, "tensor"),
        P(DP, "tensor"),
        P(DP, "tensor"),
        P(DP, "tensor", None, None, None),
        P(DP, "tensor", None, None, None),
        P(DP, "tensor", None, None, None),
    )
    return jax.shard_map(body, mesh=torus, in_specs=in_specs, out_specs=out_specs, check_vma=False)
```
